256 devices in a mesh: bulk: 16 (over z, core), wide: 16 (over y, x).
Axes of the slice: x: 4, y: 4, z: 8, core: 2. Of those that a mesh axis runs over, the one named last changes fastest.
Arguments:
- wavefunction: float32 [16384, 512], P('wide'), may hold values from -6 to 6
- env_blocks: float32 [256, 2048, 1024], P('bulk', 'wide'), may hold values from -0.1875 to 0.1875
- right_env: float32 [32, 512, 512], P('bulk'), may hold values from -0.0625 to 0.0625
- tile_sector: int32 [128], replicated, may hold values from 0 to 31, never falling along the last dimension, each value on 1 to 8 neighbouring positions
- term_charge: int32 [32], replicated, may hold values from -1 to 1
- block_home: int32 [16, 16], replicated, may hold values from 0 to 15, as said below
Outputs:
- applied: float32 [16384, 512], P('wide', 'bulk')
The draws below stay inside these ranges and needn't reach their ends.
Inputs may be any that keep to these rules, and one draw needn't show every extreme that they name: `tile_sector`: never falls; each sector 0 to 31 covers 1 to 8 whole tiles, one exactly 8. `term_charge`: each MPO term raises, keeps or lowers the left quantum number by one. For each pair index k the column block_home[:, k] is a permutation of the bulk indices, so every device stores exactly one block of each k; at most 2 blocks of one term owner lie on one device, and some device holds 2 of them.
All inputs are finite; a program needn't handle non-finite values.
Results may differ from the reference program's by a relative error of at most 0.0003.
Values sent between devices are 32-bit elements; how exact they have to be, the bound alone decides.
No kernel may reach another device: no remote copies, remote signals or barrier semaphores. Data moves between devices by JAX's collectives and lax.ppermute only.
A program may use at most 192 MiB of HBM per device.

```python
import math
import jax
import jax.numpy as jnp
import numpy as np
from jax import lax

TILE = 128
MOST = 8
COLS = 512
NW_DEV = 2
TILE_DEV = 8
SRC = 1024
PAIRS = 16
TILES = 128
SECTORS = 32
NW = 32
HOMES = 16
N_WIDE = 16


def draw_block_home(key, part):
    subkeys = jax.random.split(key, 4)
    doubled = jax.random.randint(subkeys[0], (), 0, HOMES).astype(jnp.int32)
    others = jax.random.permutation(subkeys[1], 2 * HOMES - 2)[:PAIRS - 2].astype(jnp.int32)
    values = others // 2
    values = values + (values >= doubled).astype(jnp.int32)
    offsets = jnp.concatenate([jnp.stack([doubled, doubled]), values]).astype(jnp.int32)
    offsets = offsets[jax.random.permutation(subkeys[2], PAIRS)]
    relabel = jax.random.permutation(subkeys[3], HOMES).astype(jnp.int32)
    dest_rows = jnp.arange(HOMES, dtype=jnp.int32)
    return relabel[(dest_rows[:, None] + offsets[None, :]) % HOMES].astype(jnp.int32)


def plant(values, key, smallest, high):
    extent = values.shape
    spot = [jax.random.randint(jax.random.fold_in(key, axis), (), 0, extent[axis]) for axis in range(len(extent))]
    values = values.at[tuple(spot)].set(smallest)
    longest = extent.index(max(extent))
    spot[longest] = (spot[longest] + 1) % extent[longest]
    return values.at[tuple(spot)].set(high)


def spiked(result, key, source, target, shards_of, factor):
    def block_of(axis_at):
        return (jnp.arange(result.shape[axis_at]) // (result.shape[axis_at] // shards_of)).reshape((-1,) + (1,) * (result.ndim - 1 - axis_at))

    first = jax.random.permutation(key, shards_of)[block_of(target)]
    far = (block_of(target) + shards_of // 2) % shards_of
    return jnp.where((block_of(source) == first) | (block_of(source) == far), factor * result, result)


def block_scale(rng, shape, cuts, low, top_value):
    loudness, own = 1.0, jax.random.fold_in(rng, 6)
    for position, shards_of in cuts:
        steps = jnp.exp(jax.random.uniform(jax.random.fold_in(own, position), (shards_of,), jnp.float32, low / len(cuts), top_value / len(cuts)))
        loudness = loudness * jnp.repeat(steps, shape[position] // shards_of).reshape([-1 if axis == position else 1 for axis in range(len(shape))])
    return loudness


def split_up(amount, total, bound, slope):
    weights = [(1 << 20) // math.isqrt(grade ** slope) + 1 for grade in range(2, amount + 1)]
    surplus, holding = total - bound - (amount - 1), [1] * (amount - 1)
    while surplus > 0:
        free = [i for i in range(amount - 1) if holding[i] < bound]
        pool, budget = sum([weights[i] for i in free]), surplus
        for i in free:
            extra = min(bound - holding[i], max(1, budget * weights[i] // pool), surplus)
            holding[i] = holding[i] + extra
            surplus = surplus - extra
    return np.array([bound] + holding)


def uneven(key, amount, total, bound, slope):
    if amount == 2:
        one = jax.random.randint(key, (), max(1, total - bound), min(bound, total - 1) + 1)
        return jnp.stack([one, total - one])
    sizes = jnp.asarray(split_up(amount, total, bound, slope), jnp.int32)
    twos = (amount - 1) // 2
    donor, receiver = sizes[1:1 + 2 * twos:2], sizes[2:2 + 2 * twos:2]
    slack = jnp.minimum(donor - 1, bound - receiver)
    shifted = jax.random.randint(jax.random.fold_in(key, 1), (twos,), 0, 1 << 20) % (slack + 1)
    sizes = sizes.at[1:1 + 2 * twos:2].set(donor - shifted).at[2:2 + 2 * twos:2].set(receiver + shifted)
    return sizes[jax.random.permutation(jax.random.fold_in(key, 2), amount)]


def bell_draw(stream_key, dims, scale, limit, shards=(), kind=jnp.bfloat16):
    values = scale * jax.random.normal(stream_key, dims, jnp.float32)
    if shards:
        values = values * block_scale(stream_key, dims, shards, -0.22, 0.18)
    return jnp.clip(values, -limit, limit).astype(kind)


def bell_draw_with(rng, shape, deviation, reach, pieces, heavy, held_as=jnp.bfloat16):
    values = deviation * jax.random.normal(rng, shape, jnp.float32)
    if pieces:
        values = values * block_scale(rng, shape, pieces, -0.22, 0.18)
    return jnp.clip(spiked(values, jax.random.fold_in(rng, 3), *heavy), -reach, reach).astype(held_as)


def setup_inputs(seed: int = 0) -> dict:
    keys = jax.random.split(jax.random.key(seed), 7)
    return {
        "wavefunction": bell_draw(keys[0], (TILES * TILE, COLS), 1.0, 6.0, ((0, 16),), jnp.float32),
        "env_blocks": bell_draw(keys[1], (HOMES * PAIRS, N_WIDE * TILE, SRC), SRC ** -0.5, 0.1875, ((0, 16), (1, 16)), jnp.float32),
        "right_env": bell_draw_with(keys[2], (NW, COLS, COLS), (COLS * NW) ** -0.5, 0.0625, ((0, 16),), (0, 2, 16, 2.0), jnp.float32),
        "tile_sector": jnp.searchsorted(jnp.cumsum(uneven(keys[3], SECTORS, TILES, MOST, 2)), jnp.arange(TILES), side="right").astype(jnp.int32),
        "term_charge": plant(jax.random.randint(keys[4], (NW,), -1, 2), jax.random.fold_in(keys[4], 1), -1, 1).astype(jnp.int32),
        "block_home": draw_block_home(jax.random.fold_in(keys[6], 71), 0),
    }


precise = lax.Precision.HIGHEST


def reference(wavefunction, env_blocks, right_env, tile_sector, term_charge, block_home):
    labels = jnp.arange(TILES, dtype=jnp.int32)
    starts = jnp.sum((tile_sector[None, :] < labels[:, None]).astype(jnp.int32), axis=1)
    widths = jnp.sum((tile_sector[None, :] == labels[:, None]).astype(jnp.int32), axis=1)
    sectors = tile_sector[TILES - 1] + 1
    window_rows = jnp.arange(SRC, dtype=jnp.int32)
    padded = jnp.concatenate([wavefunction, jnp.zeros((SRC, COLS), wavefunction.dtype)], axis=0)

    def one_tile(tile_index):
        column = tile_index // TILE_DEV
        within = tile_index % TILE_DEV

        def add_term(term_index, total):
            term_index = jnp.asarray(term_index).astype(jnp.int32)
            holder = term_index // NW_DEV
            slot_index = within * NW_DEV + term_index % NW_DEV
            stored_at = block_home[holder, slot_index]
            source = tile_sector[tile_index] + term_charge[term_index]
            usable = (source >= 0) & (source < sectors)
            clipped = jnp.clip(source, 0, TILES - 1)
            live_rows = jnp.where(usable, widths[clipped] * TILE, 0)
            window = lax.dynamic_slice(padded, ((starts[clipped] * TILE).astype(jnp.int32), jnp.int32(0)), (SRC, COLS))
            window = jnp.where((window_rows < live_rows)[:, None], window, 0.0)
            env_block = lax.dynamic_slice(env_blocks, ((stored_at * PAIRS + slot_index).astype(jnp.int32), (column * TILE).astype(jnp.int32), jnp.int32(0)), (1, TILE, SRC))[0]
            left_part = jnp.dot(env_block, window, precision=precise, preferred_element_type=jnp.float32)
            return total + jnp.dot(left_part, right_env[term_index], precision=precise, preferred_element_type=jnp.float32)

        return lax.fori_loop(0, NW, add_term, jnp.zeros((TILE, COLS), jnp.float32))

    return lax.map(one_tile, labels).reshape(TILES * TILE, COLS)
```

```python
import jax
import jax.numpy as jnp
from jax import lax
from jax.experimental import pallas as pl
from jax.experimental.pallas import tpu as pltpu
from jax.sharding import Mesh, PartitionSpec as P

TILE = 128
COLS = 512
HALF = COLS // 2
TILE_DEV = 8
SRC = 1024
PAIRS = 16
HOMES = 16
REACH = 2
SLABS = 2 * REACH + 1
ROWS = TILE_DEV * TILE
PART = ROWS // HOMES
SUB = 32
VMEM = 56 * 1024 * 1024

START, COUNT, TERM, CORE, PX, PY = 0, 16, 32, 48, 49, 50


def split(value):
    high = value.astype(jnp.bfloat16)
    low = (value - high.astype(jnp.float32)).astype(jnp.bfloat16)
    return high, low


def product(left, high, low):
    left_high, left_low = split(left)
    rows = left.shape[0]
    both = jnp.dot(
        jnp.concatenate([left_high, left_low], axis=0), high, preferred_element_type=jnp.float32
    )
    rest = jnp.dot(left_high, low, preferred_element_type=jnp.float32)
    return both[:rows] + both[rows:] + rest


def left_kernel(plan, own, near, env_own, env_other, out, high, low):
    pair = pl.program_id(0)

    @pl.when(pair == 0)
    def _():
        def put(row, value):
            spot = pl.ds(pl.multiple_of(row, PART), PART)
            high[spot, :], low[spot, :] = split(value)

        @pl.loop(0, HOMES)
        def _(home):
            for at, slab in enumerate(s for s in range(SLABS) if s != REACH):
                put(slab * ROWS + home * PART, near[home, at])
            put(REACH * ROWS + home * PART, own[pl.ds(pl.multiple_of(home * PART, PART), PART), :])

        tail = jnp.zeros((2 * TILE, COLS), jnp.bfloat16)
        high[SLABS * ROWS :, :] = tail
        low[SLABS * ROWS :, :] = tail

    def contract(env):
        first, count = plan[START + pair], plan[COUNT + pair]
        out[0] = jnp.zeros((TILE, COLS), jnp.float32)

        def chunk(step, carry):
            block = env[0, :, pl.ds(pl.multiple_of(step * 2 * TILE, 2 * TILE), 2 * TILE)]
            column = step * 2 * TILE + lax.broadcasted_iota(jnp.int32, block.shape, 1)
            block = jnp.where(column < count * TILE, block, 0.0)
            spot = pl.ds(pl.multiple_of((first + 2 * step) * TILE, TILE), 2 * TILE)
            out[0] += product(block, high[spot, :], low[spot, :])
            return carry

        lax.fori_loop(0, (count + 1) // 2, chunk, 0)

    @pl.when(pair % 2 == 0)
    def _():
        contract(env_own)

    @pl.when(pair % 2 == 1)
    def _():
        contract(env_other)


def left_products(plan, own, near, env, env_other):
    grid = pltpu.PrefetchScalarGridSpec(
        num_scalar_prefetch=1,
        grid=(PAIRS,),
        in_specs=[
            pl.BlockSpec((ROWS, COLS), lambda p, plan: (0, 0), pipeline_mode=pl.Buffered(1)),
            pl.BlockSpec(near.shape, lambda p, plan: (0, 0, 0, 0), pipeline_mode=pl.Buffered(1)),
            pl.BlockSpec((1, TILE, SRC), lambda p, plan: ((p // 2) * 2 + plan[CORE], 0, 0)),
            pl.BlockSpec((1, TILE, SRC), lambda p, plan: (p // 2, 0, 0)),
        ],
        out_specs=pl.BlockSpec((1, TILE, COLS), lambda p, plan: (p, 0, 0)),
        scratch_shapes=[pltpu.VMEM((SLABS * ROWS + 2 * TILE, COLS), jnp.bfloat16)] * 2,
    )
    return pl.pallas_call(
        left_kernel,
        grid_spec=grid,
        out_shape=jax.ShapeDtypeStruct((PAIRS, TILE, COLS), jnp.float32),
        compiler_params=pltpu.CompilerParams(vmem_limit_bytes=VMEM),
        cost_estimate=pl.CostEstimate(
            flops=6 * PAIRS * TILE * SRC * COLS, bytes_accessed=24 << 20, transcendentals=0
        ),
        name="left_products",
    )(plan, own, near, env, env_other)


def right_kernel(plan, left, *refs):
    parts, (keep, send, total, *halves) = refs[:10], refs[10:]
    pair = pl.program_id(0)
    core, x, y = plan[CORE], plan[PX], plan[PY]
    value = []
    for half, (major, minor) in enumerate(((y, x), (x, y))):
        here, after, across_low, across_high, before = parts[5 * half : 5 * half + 5]
        high, low = halves[2 * half : 2 * half + 2]
        pieces = [
            [here.at[i] for i in range(4)],
            [after.at[i] for i in range(4)],
            [across_low.at[0], across_low.at[1], across_high.at[0], across_high.at[1]],
            [before.at[i] for i in range(4)],
        ]
        lefts = []
        for r in range(4):
            for i in range(4):
                spot = pl.ds(pl.multiple_of(r * TILE + ((minor + i) % 4) * SUB, SUB), SUB)
                high[spot, :], low[spot, :] = split(pieces[r][i][0])
            lefts.append(left[0, :, pl.ds(pl.multiple_of(((major + r) % 4) * TILE, TILE), TILE)])
        value.append(product(jnp.concatenate(lefts, axis=1), high[...], low[...]))
    value = jnp.concatenate(value, axis=1)

    @pl.when(pair % 2 == 0)
    def _():
        total[...] = value

    @pl.when(pair % 2 == 1)
    def _():
        turned = (total[...] + value).T.reshape(HOMES // 2, 2, SUB, TILE)
        keep[...] = jnp.where(core == 0, turned[:, 0], turned[:, 1])
        send[...] = jnp.where(core == 0, turned[:, 1], turned[:, 0])


def right_products(plan, left, parts):
    def part_spec(part):
        return pl.BlockSpec((part.shape[0], 1, SUB, HALF), lambda p, plan: (0, plan[TERM + p], 0, 0))

    out = jax.ShapeDtypeStruct((HOMES // 2, SUB, ROWS), jnp.float32)
    out_spec = pl.BlockSpec((HOMES // 2, SUB, TILE), lambda p, plan: (0, 0, p // 2))
    grid = pltpu.PrefetchScalarGridSpec(
        num_scalar_prefetch=1,
        grid=(PAIRS,),
        in_specs=[pl.BlockSpec((1, TILE, COLS), lambda p, plan: (p, 0, 0))]
        + [part_spec(part) for part in parts],
        out_specs=[out_spec, out_spec],
        scratch_shapes=[pltpu.VMEM((TILE, COLS), jnp.float32)]
        + [pltpu.VMEM((COLS, HALF), jnp.bfloat16)] * 4,
    )
    return pl.pallas_call(
        right_kernel,
        grid_spec=grid,
        out_shape=[out, out],
        compiler_params=pltpu.CompilerParams(vmem_limit_bytes=VMEM),
        cost_estimate=pl.CostEstimate(
            flops=6 * PAIRS * TILE * COLS * COLS, bytes_accessed=22 << 20, transcendentals=0
        ),
        name="right_products",
    )(plan, left, *parts)


def ring(value, axis, steps):
    count = lax.axis_size(axis)
    return lax.ppermute(value, axis, [(i, (i - steps) % count) for i in range(count)])


def around(value, axis, cut):
    after, before = ring(value, axis, 1), ring(value, axis, -1)
    low = ring(lax.slice_in_dim(after, 0, cut), axis, 1)
    high = ring(lax.slice_in_dim(before, cut, value.shape[0]), axis, -1)
    return value, after, low, high, before


def wide_shift(value, steps):
    count = lax.axis_size(("y", "x"))
    return lax.ppermute(
        value, ("y", "x"), [(i, i + steps) for i in range(max(0, -steps), min(count, count - steps))]
    )


def make_plan(tile_sector, term_charge, block_home, home, core, x, y):
    base = (y * 4 + x) * TILE_DEV
    paired = block_home.reshape(HOMES, TILE_DEV, 2)
    mine = jnp.where(core == 0, paired[:, :, 0], paired[:, :, 1])
    homes = home + jnp.arange(2, dtype=jnp.int32) * (1 - 2 * core)
    owner_ids = jnp.arange(HOMES, dtype=jnp.int32)[:, None, None]
    owner = jnp.sum(
        jnp.where(mine[:, :, None] == homes[None, None, :], owner_ids, 0), axis=0
    ).reshape(PAIRS)
    term = owner * 2 + core
    term_ids = jnp.arange(2 * HOMES, dtype=jnp.int32)
    charge = jnp.sum(jnp.where(term[:, None] == term_ids[None, :], term_charge[None, :], 0), axis=1)
    tiles = lax.dynamic_slice(tile_sector, (base,), (TILE_DEV,))
    source = jnp.broadcast_to(tiles[:, None], (TILE_DEV, 2)).reshape(PAIRS) + charge
    usable = (source >= 0) & (source <= tile_sector[-1])
    first = jnp.sum((tile_sector[None, :] < source[:, None]).astype(jnp.int32), axis=1)
    count = jnp.sum((tile_sector[None, :] == source[:, None]).astype(jnp.int32), axis=1)
    first = jnp.where(usable, first - (base - REACH * TILE_DEV), 0)
    count = jnp.where(usable, count, 0)
    return jnp.concatenate([first, count, owner, jnp.stack([core, x, y])]).astype(jnp.int32)


def on_device(wavefunction, env_blocks, right_env, tile_sector, term_charge, block_home):
    z, core = lax.axis_index("z"), lax.axis_index("core")
    y, x = lax.axis_index("y"), lax.axis_index("x")
    home = 2 * z + core
    swap = [(0, 1), (1, 0)]

    by_y = lax.dynamic_slice(right_env, (0, y * TILE + x * SUB, 0), (2, SUB, HALF))
    by_x = lax.dynamic_slice(right_env, (0, x * TILE + y * SUB, HALF), (2, SUB, HALF))
    column = lax.all_gather(jnp.stack([by_y, by_x], axis=1), ("z", "core"))

    strip = lax.dynamic_slice(wavefunction, (home * PART, 0), (PART, COLS))
    near = jnp.stack([wide_shift(strip, steps) for steps in (2, 1, -1, -2)])
    near = lax.all_gather(near, ("z", "core"))

    paired = env_blocks.reshape(TILE_DEV, 2, TILE, SRC)
    env_other = lax.ppermute(
        lax.dynamic_index_in_dim(paired, 1 - core, axis=1, keepdims=False), "core", swap
    )
    plan = make_plan(tile_sector, term_charge, block_home, home, core, x, y)

    mine = lax.dynamic_index_in_dim(column, core, axis=1, keepdims=False)
    parts = []
    for at, (first, then) in enumerate((("x", "y"), ("y", "x"))):
        here, after, low, high, before = around(mine[:, at], first, HOMES // 2)
        gathered = jnp.stack([here, after, jnp.concatenate([low, high], axis=0), before])
        parts += around(gathered, then, 2)

    left = left_products(plan, wavefunction, near, env_blocks, env_other)
    keep, send = right_products(plan, left, parts)
    total = keep + lax.ppermute(send, "core", swap)
    shares = lax.all_to_all(total, "z", split_axis=0, concat_axis=0, tiled=True)
    shares = shares.reshape(HOMES // 2, SUB, ROWS)
    return jnp.sum(shares, axis=0).T


def solution(mesh):
    fine = Mesh(mesh.devices.reshape(8, 2, 4, 4), ("z", "core", "y", "x"))
    bulk, wide = ("z", "core"), ("y", "x")
    return jax.shard_map(
        on_device,
        mesh=fine,
        in_specs=(P(wide, None), P(bulk, wide, None), P(bulk, None, None), P(), P(), P()),
        out_specs=P(wide, bulk),
        check_vma=False,
    )
```

```python
import jax
import jax.numpy as jnp
from jax import lax
from jax.experimental import pallas as pl
from jax.experimental.pallas import tpu as pltpu
from jax.sharding import Mesh, PartitionSpec as P

TILE = 128
COLS = 512
HALF = COLS // 2
TILE_DEV = 8
SRC = 1024
PAIRS = 16
HOMES = 16
REACH = 2
SLABS = 2 * REACH + 1
ROWS = TILE_DEV * TILE
PART = ROWS // HOMES
SUB = 32
VMEM = 56 * 1024 * 1024

START, COUNT, TERM, CORE, PX, PY = 0, 16, 32, 48, 49, 50


def split(value):
    high = value.astype(jnp.bfloat16)
    low = (value - high.astype(jnp.float32)).astype(jnp.bfloat16)
    return high, low


def product(left, high, low):
    left_high, left_low = split(left)
    rows = left.shape[0]
    both = jnp.dot(
        jnp.concatenate([left_high, left_low], axis=0), high, preferred_element_type=jnp.float32
    )
    rest = jnp.dot(left_high, low, preferred_element_type=jnp.float32)
    return both[:rows] + both[rows:] + rest


def left_kernel(plan, own, near, env_own, env_other, out, high, low):
    pair = pl.program_id(0)

    @pl.when(pair == 0)
    def _():
        def put(row, value):
            spot = pl.ds(pl.multiple_of(row, PART), PART)
            high[spot, :], low[spot, :] = split(value)

        @pl.loop(0, HOMES)
        def _(home):
            for at, slab in enumerate(s for s in range(SLABS) if s != REACH):
                put(slab * ROWS + home * PART, near[home, at])
            put(REACH * ROWS + home * PART, own[pl.ds(pl.multiple_of(home * PART, PART), PART), :])

        tail = jnp.zeros((2 * TILE, COLS), jnp.bfloat16)
        high[SLABS * ROWS :, :] = tail
        low[SLABS * ROWS :, :] = tail

    def contract(env):
        first, count = plan[START + pair], plan[COUNT + pair]
        out[0] = jnp.zeros((TILE, COLS), jnp.float32)

        def chunk(step, carry):
            block = env[0, :, pl.ds(pl.multiple_of(step * 2 * TILE, 2 * TILE), 2 * TILE)]
            column = step * 2 * TILE + lax.broadcasted_iota(jnp.int32, block.shape, 1)
            block = jnp.where(column < count * TILE, block, 0.0)
            spot = pl.ds(pl.multiple_of((first + 2 * step) * TILE, TILE), 2 * TILE)
            out[0] += product(block, high[spot, :], low[spot, :])
            return carry

        lax.fori_loop(0, (count + 1) // 2, chunk, 0)

    @pl.when(pair % 2 == 0)
    def _():
        contract(env_own)

    @pl.when(pair % 2 == 1)
    def _():
        contract(env_other)


def left_products(plan, own, near, env, env_other):
    grid = pltpu.PrefetchScalarGridSpec(
        num_scalar_prefetch=1,
        grid=(PAIRS,),
        in_specs=[
            pl.BlockSpec((ROWS, COLS), lambda p, plan: (0, 0), pipeline_mode=pl.Buffered(1)),
            pl.BlockSpec(near.shape, lambda p, plan: (0, 0, 0, 0), pipeline_mode=pl.Buffered(1)),
            pl.BlockSpec((1, TILE, SRC), lambda p, plan: ((p // 2) * 2 + plan[CORE], 0, 0)),
            pl.BlockSpec((1, TILE, SRC), lambda p, plan: (p // 2, 0, 0)),
        ],
        out_specs=pl.BlockSpec((1, TILE, COLS), lambda p, plan: (p, 0, 0)),
        scratch_shapes=[pltpu.VMEM((SLABS * ROWS + 2 * TILE, COLS), jnp.bfloat16)] * 2,
    )
    return pl.pallas_call(
        left_kernel,
        grid_spec=grid,
        out_shape=jax.ShapeDtypeStruct((PAIRS, TILE, COLS), jnp.float32),
        compiler_params=pltpu.CompilerParams(vmem_limit_bytes=VMEM),
        cost_estimate=pl.CostEstimate(
            flops=6 * PAIRS * TILE * SRC * COLS, bytes_accessed=24 << 20, transcendentals=0
        ),
        name="left_products",
    )(plan, own, near, env, env_other)


def gather_left(left, major, steps):
    return [
        left[pair, :, pl.ds(pl.multiple_of(((major + r) % 4) * TILE, TILE), TILE)]
        for pair in range(2)
        for r in steps
    ]


def multiply(plan, left, parts, halves, steps):
    per_half = 4 * len(steps)
    value = []
    for half, (major, minor) in enumerate(((plan[PY], plan[PX]), (plan[PX], plan[PY]))):
        high, low = halves[2 * half : 2 * half + 2]
        strips = parts[per_half * half : per_half * half + per_half]
        for pair in range(2):
            for at in range(len(steps)):
                for i in range(4):
                    strip = strips[(pair * len(steps) + at) * 2 + i // 2][i % 2, 0]
                    row = (pair * len(steps) + at) * TILE + ((minor + i) % 4) * SUB
                    spot = pl.ds(pl.multiple_of(row, SUB), SUB)
                    high[spot, :], low[spot, :] = split(strip)
        lefts = jnp.concatenate(gather_left(left, major, steps), axis=1)
        value.append(product(lefts, high[...], low[...]))
    return jnp.concatenate(value, axis=1)


NEAR_STEPS, FAR_STEPS = (0, 1, 3), (2,)


def first_kernel(plan, left, *refs):
    count = 8 * len(NEAR_STEPS)
    refs[count][0] = multiply(plan, left, refs[:count], refs[count + 1 :], NEAR_STEPS)


def second_kernel(plan, left, part, *refs):
    count = 8 * len(FAR_STEPS)
    keep, send = refs[count : count + 2]
    total = part[0] + multiply(plan, left, refs[:count], refs[count + 2 :], FAR_STEPS)
    turned = total.T.reshape(HOMES // 2, 2, SUB, TILE)
    keep[...] = jnp.where(plan[CORE] == 0, turned[:, 0], turned[:, 1])
    send[...] = jnp.where(plan[CORE] == 0, turned[:, 1], turned[:, 0])


def pair_specs(parts, steps):
    specs, arrays = [], []
    for half in parts:
        for pair in range(2):
            for step in steps:
                for array in half[step]:
                    specs.append(
                        pl.BlockSpec(
                            (2, 1, SUB, HALF),
                            lambda t, plan, pair=pair: (0, plan[TERM + 2 * t + pair], 0, 0),
                        )
                    )
                    arrays.append(array)
    return specs, arrays


def right_products(plan, left, parts):
    left_spec = pl.BlockSpec((2, TILE, COLS), lambda t, plan: (t, 0, 0))
    tile_spec = pl.BlockSpec((1, TILE, COLS), lambda t, plan: (t, 0, 0))

    def cost(steps):
        return pl.CostEstimate(
            flops=6 * PAIRS * TILE * COLS * TILE * len(steps),
            bytes_accessed=(6 + 4 * len(steps)) << 20,
            transcendentals=0,
        )

    def scratch(steps):
        return [pltpu.VMEM((2 * len(steps) * TILE, HALF), jnp.bfloat16)] * 4

    specs, arrays = pair_specs(parts, NEAR_STEPS)
    first = pl.pallas_call(
        first_kernel,
        grid_spec=pltpu.PrefetchScalarGridSpec(
            num_scalar_prefetch=1,
            grid=(TILE_DEV,),
            in_specs=[left_spec] + specs,
            out_specs=tile_spec,
            scratch_shapes=scratch(NEAR_STEPS),
        ),
        out_shape=jax.ShapeDtypeStruct((TILE_DEV, TILE, COLS), jnp.float32),
        compiler_params=pltpu.CompilerParams(vmem_limit_bytes=VMEM),
        cost_estimate=cost(NEAR_STEPS),
        name="right_near",
    )(plan, left, *arrays)
    specs, arrays = pair_specs(parts, FAR_STEPS)
    out = jax.ShapeDtypeStruct((HOMES // 2, SUB, ROWS), jnp.float32)
    out_spec = pl.BlockSpec((HOMES // 2, SUB, TILE), lambda t, plan: (0, 0, t))
    return pl.pallas_call(
        second_kernel,
        grid_spec=pltpu.PrefetchScalarGridSpec(
            num_scalar_prefetch=1,
            grid=(TILE_DEV,),
            in_specs=[left_spec, tile_spec] + specs,
            out_specs=[out_spec, out_spec],
            scratch_shapes=scratch(FAR_STEPS),
        ),
        out_shape=[out, out],
        compiler_params=pltpu.CompilerParams(vmem_limit_bytes=VMEM),
        cost_estimate=cost(FAR_STEPS),
        name="right_far",
    )(plan, left, first, *arrays)


def ring(value, axis, steps):
    count = lax.axis_size(axis)
    return lax.ppermute(value, axis, [(i, (i - steps) % count) for i in range(count)])


def around(value, axis, cut):
    after, before = ring(value, axis, 1), ring(value, axis, -1)
    low = ring(lax.slice_in_dim(after, 0, cut), axis, 1)
    high = ring(lax.slice_in_dim(before, cut, value.shape[0]), axis, -1)
    return value, after, low, high, before


def wide_shift(value, steps):
    count = lax.axis_size(("y", "x"))
    return lax.ppermute(
        value, ("y", "x"), [(i, i + steps) for i in range(max(0, -steps), min(count, count - steps))]
    )


def make_plan(tile_sector, term_charge, block_home, home, core, x, y):
    base = (y * 4 + x) * TILE_DEV
    paired = block_home.reshape(HOMES, TILE_DEV, 2)
    mine = jnp.where(core == 0, paired[:, :, 0], paired[:, :, 1])
    homes = home + jnp.arange(2, dtype=jnp.int32) * (1 - 2 * core)
    owner_ids = jnp.arange(HOMES, dtype=jnp.int32)[:, None, None]
    owner = jnp.sum(
        jnp.where(mine[:, :, None] == homes[None, None, :], owner_ids, 0), axis=0
    ).reshape(PAIRS)
    term = owner * 2 + core
    term_ids = jnp.arange(2 * HOMES, dtype=jnp.int32)
    charge = jnp.sum(jnp.where(term[:, None] == term_ids[None, :], term_charge[None, :], 0), axis=1)
    tiles = lax.dynamic_slice(tile_sector, (base,), (TILE_DEV,))
    source = jnp.broadcast_to(tiles[:, None], (TILE_DEV, 2)).reshape(PAIRS) + charge
    usable = (source >= 0) & (source <= tile_sector[-1])
    first = jnp.sum((tile_sector[None, :] < source[:, None]).astype(jnp.int32), axis=1)
    count = jnp.sum((tile_sector[None, :] == source[:, None]).astype(jnp.int32), axis=1)
    first = jnp.where(usable, first - (base - REACH * TILE_DEV), 0)
    count = jnp.where(usable, count, 0)
    slot = (owner // 2) * 2 + (owner + core) % 2
    return jnp.concatenate([first, count, slot, jnp.stack([core, x, y])]).astype(jnp.int32)


def on_device(wavefunction, env_blocks, right_env, tile_sector, term_charge, block_home):
    z, core = lax.axis_index("z"), lax.axis_index("core")
    y, x = lax.axis_index("y"), lax.axis_index("x")
    home = 2 * z + core
    swap = [(0, 1), (1, 0)]

    by_y = lax.dynamic_slice(right_env, (0, y * TILE + x * SUB, 0), (2, SUB, HALF))
    by_x = lax.dynamic_slice(right_env, (0, x * TILE + y * SUB, HALF), (2, SUB, HALF))
    strips = jnp.stack([by_y, by_x], axis=1)
    kept = lax.dynamic_index_in_dim(strips, core, axis=0, keepdims=False)
    given = lax.dynamic_index_in_dim(strips, 1 - core, axis=0, keepdims=False)
    column = lax.all_gather(jnp.stack([kept, lax.ppermute(given, "core", swap)]), "z")
    column = column.reshape(HOMES, 2, SUB, HALF)

    strip = lax.dynamic_slice(wavefunction, (home * PART, 0), (PART, COLS))
    near = jnp.stack([wide_shift(strip, steps) for steps in (2, 1, -1, -2)])
    near = lax.all_gather(near, ("z", "core"))

    paired = env_blocks.reshape(TILE_DEV, 2, TILE, SRC)
    env_other = lax.ppermute(
        lax.dynamic_index_in_dim(paired, 1 - core, axis=1, keepdims=False), "core", swap
    )
    plan = make_plan(tile_sector, term_charge, block_home, home, core, x, y)

    parts = []
    for at, (first, then) in enumerate((("x", "y"), ("y", "x"))):
        here, after, low, high, before = around(column[:, at], first, HOMES // 2)
        ahead = jnp.stack([here, after])
        behind = jnp.stack([jnp.concatenate([low, high], axis=0), before])
        ahead_after, behind_before = ring(ahead, then, 1), ring(behind, then, -1)
        behind_after, ahead_before = ring(behind, then, 1), ring(ahead, then, -1)
        across = ring(ahead_after, then, 1), ring(behind_before, then, -1)
        parts.append(
            ((ahead, behind), (ahead_after, behind_after), across, (ahead_before, behind_before))
        )

    left = left_products(plan, wavefunction, near, env_blocks, env_other)
    keep, send = right_products(plan, left, parts)
    total = keep + lax.ppermute(send, "core", swap)
    shares = lax.all_to_all(total, "z", split_axis=0, concat_axis=0, tiled=True)
    shares = shares.reshape(HOMES // 2, SUB, ROWS)
    return jnp.sum(shares, axis=0).T


def solution(mesh):
    fine = Mesh(mesh.devices.reshape(8, 2, 4, 4), ("z", "core", "y", "x"))
    bulk, wide = ("z", "core"), ("y", "x")
    return jax.shard_map(
        on_device,
        mesh=fine,
        in_specs=(P(wide, None), P(bulk, wide, None), P(bulk, None, None), P(), P(), P()),
        out_specs=P(wide, bulk),
        check_vma=False,
    )
```

```python
import jax
import jax.numpy as jnp
from jax import lax
from jax.experimental import pallas as pl
from jax.experimental.pallas import tpu as pltpu
from jax.sharding import Mesh, PartitionSpec as P

TILE = 128
COLS = 512
HALF = COLS // 2
TILE_DEV = 8
SRC = 1024
PAIRS = 16
HOMES = 16
REACH = 2
SLABS = 2 * REACH + 1
ROWS = TILE_DEV * TILE
PART = ROWS // HOMES
SUB = 32
VMEM = 56 * 1024 * 1024

START, COUNT, TERM, CORE, PX, PY = 0, 16, 32, 48, 49, 50


def split(value):
    high = value.astype(jnp.bfloat16)
    low = (value - high.astype(jnp.float32)).astype(jnp.bfloat16)
    return high, low


def product(left, high, low):
    left_high, left_low = split(left)
    rows = left.shape[0]
    both = jnp.dot(
        jnp.concatenate([left_high, left_low], axis=0), high, preferred_element_type=jnp.float32
    )
    rest = jnp.dot(left_high, low, preferred_element_type=jnp.float32)
    return both[:rows] + both[rows:] + rest


def left_kernel(plan, own, near, env_own, env_other, out, high, low):
    pair = pl.program_id(0)

    @pl.when(pair == 0)
    def _():
        def put(row, value):
            spot = pl.ds(pl.multiple_of(row, PART), PART)
            high[spot, :], low[spot, :] = split(value)

        @pl.loop(0, HOMES)
        def _(home):
            for at, slab in enumerate(s for s in range(SLABS) if s != REACH):
                put(slab * ROWS + home * PART, near[home, at])
            put(REACH * ROWS + home * PART, own[pl.ds(pl.multiple_of(home * PART, PART), PART), :])

        tail = jnp.zeros((2 * TILE, COLS), jnp.bfloat16)
        high[SLABS * ROWS :, :] = tail
        low[SLABS * ROWS :, :] = tail

    def contract(env):
        first, count = plan[START + pair], plan[COUNT + pair]
        out[0] = jnp.zeros((TILE, COLS), jnp.float32)

        def chunk(step, carry):
            block = env[0, :, pl.ds(pl.multiple_of(step * 2 * TILE, 2 * TILE), 2 * TILE)]
            column = step * 2 * TILE + lax.broadcasted_iota(jnp.int32, block.shape, 1)
            block = jnp.where(column < count * TILE, block, 0.0)
            spot = pl.ds(pl.multiple_of((first + 2 * step) * TILE, TILE), 2 * TILE)
            out[0] += product(block, high[spot, :], low[spot, :])
            return carry

        lax.fori_loop(0, (count + 1) // 2, chunk, 0)

    @pl.when(pair % 2 == 0)
    def _():
        contract(env_own)

    @pl.when(pair % 2 == 1)
    def _():
        contract(env_other)


def left_products(plan, own, near, env, env_other):
    grid = pltpu.PrefetchScalarGridSpec(
        num_scalar_prefetch=1,
        grid=(PAIRS,),
        in_specs=[
            pl.BlockSpec((ROWS, COLS), lambda p, plan: (0, 0), pipeline_mode=pl.Buffered(1)),
            pl.BlockSpec(near.shape, lambda p, plan: (0, 0, 0, 0), pipeline_mode=pl.Buffered(1)),
            pl.BlockSpec((1, TILE, SRC), lambda p, plan: ((p // 2) * 2 + plan[CORE], 0, 0)),
            pl.BlockSpec((1, TILE, SRC), lambda p, plan: (p // 2, 0, 0)),
        ],
        out_specs=pl.BlockSpec((1, TILE, COLS), lambda p, plan: (p, 0, 0)),
        scratch_shapes=[pltpu.VMEM((SLABS * ROWS + 2 * TILE, COLS), jnp.bfloat16)] * 2,
    )
    return pl.pallas_call(
        left_kernel,
        grid_spec=grid,
        out_shape=jax.ShapeDtypeStruct((PAIRS, TILE, COLS), jnp.float32),
        compiler_params=pltpu.CompilerParams(vmem_limit_bytes=VMEM),
        cost_estimate=pl.CostEstimate(
            flops=6 * PAIRS * TILE * SRC * COLS, bytes_accessed=24 << 20, transcendentals=0
        ),
        name="left_products",
    )(plan, own, near, env, env_other)


def gather_left(left, major, steps):
    return [
        left[pair, :, pl.ds(pl.multiple_of(((major + r) % 4) * TILE, TILE), TILE)]
        for pair in range(2)
        for r in steps
    ]


def multiply(plan, left, parts, halves, steps):
    per_half = 4 * len(steps)
    value = []
    for half, (major, minor) in enumerate(((plan[PY], plan[PX]), (plan[PX], plan[PY]))):
        high, low = halves[2 * half : 2 * half + 2]
        strips = parts[per_half * half : per_half * half + per_half]
        for pair in range(2):
            for at in range(len(steps)):
                for i in range(4):
                    strip = strips[(pair * len(steps) + at) * 2 + i // 2][i % 2, 0]
                    row = (pair * len(steps) + at) * TILE + ((minor + i) % 4) * SUB
                    spot = pl.ds(pl.multiple_of(row, SUB), SUB)
                    high[spot, :], low[spot, :] = split(strip)
        lefts = jnp.concatenate(gather_left(left, major, steps), axis=1)
        value.append(product(lefts, high[...], low[...]))
    return jnp.concatenate(value, axis=1)


NEAR_STEPS, FAR_STEPS = (0, 1, 3), (2,)


def first_kernel(plan, left, *refs):
    count = 8 * len(NEAR_STEPS)
    refs[count][0] = multiply(plan, left, refs[:count], refs[count + 1 :], NEAR_STEPS)


def second_kernel(plan, left, part, *refs):
    count = 8 * len(FAR_STEPS)
    keep, send = refs[count : count + 2]
    total = part[0] + multiply(plan, left, refs[:count], refs[count + 2 :], FAR_STEPS)
    turned = total.T.reshape(HOMES // 2, 2, SUB, TILE)
    keep[...] = jnp.where(plan[CORE] == 0, turned[:, 0], turned[:, 1])
    send[...] = jnp.where(plan[CORE] == 0, turned[:, 1], turned[:, 0])


def pair_specs(parts, steps):
    specs, arrays = [], []
    for half in parts:
        for pair in range(2):
            for step in steps:
                for array in half[step]:
                    specs.append(
                        pl.BlockSpec(
                            (2, 1, SUB, HALF),
                            lambda t, plan, pair=pair: (0, plan[TERM + 2 * t + pair], 0, 0),
                        )
                    )
                    arrays.append(array)
    return specs, arrays


def right_products(plan, left, parts):
    left_spec = pl.BlockSpec((2, TILE, COLS), lambda t, plan: (t, 0, 0))
    tile_spec = pl.BlockSpec((1, TILE, COLS), lambda t, plan: (t, 0, 0))

    def cost(steps):
        return pl.CostEstimate(
            flops=6 * PAIRS * TILE * COLS * TILE * len(steps),
            bytes_accessed=(6 + 4 * len(steps)) << 20,
            transcendentals=0,
        )

    def scratch(steps):
        return [pltpu.VMEM((2 * len(steps) * TILE, HALF), jnp.bfloat16)] * 4

    specs, arrays = pair_specs(parts, NEAR_STEPS)
    first = pl.pallas_call(
        first_kernel,
        grid_spec=pltpu.PrefetchScalarGridSpec(
            num_scalar_prefetch=1,
            grid=(TILE_DEV,),
            in_specs=[left_spec] + specs,
            out_specs=tile_spec,
            scratch_shapes=scratch(NEAR_STEPS),
        ),
        out_shape=jax.ShapeDtypeStruct((TILE_DEV, TILE, COLS), jnp.float32),
        compiler_params=pltpu.CompilerParams(vmem_limit_bytes=VMEM),
        cost_estimate=cost(NEAR_STEPS),
        name="right_near",
    )(plan, left, *arrays)
    specs, arrays = pair_specs(parts, FAR_STEPS)
    out = jax.ShapeDtypeStruct((HOMES // 2, SUB, ROWS), jnp.float32)
    out_spec = pl.BlockSpec((HOMES // 2, SUB, TILE), lambda t, plan: (0, 0, t))
    return pl.pallas_call(
        second_kernel,
        grid_spec=pltpu.PrefetchScalarGridSpec(
            num_scalar_prefetch=1,
            grid=(TILE_DEV,),
            in_specs=[left_spec, tile_spec] + specs,
            out_specs=[out_spec, out_spec],
            scratch_shapes=scratch(FAR_STEPS),
        ),
        out_shape=[out, out],
        compiler_params=pltpu.CompilerParams(vmem_limit_bytes=VMEM),
        cost_estimate=cost(FAR_STEPS),
        name="right_far",
    )(plan, left, first, *arrays)


def ring(value, axis, steps):
    count = lax.axis_size(axis)
    return lax.ppermute(value, axis, [(i, (i - steps) % count) for i in range(count)])


def around(value, axis, cut):
    after, before = ring(value, axis, 1), ring(value, axis, -1)
    low = ring(lax.slice_in_dim(after, 0, cut), axis, 1)
    high = ring(lax.slice_in_dim(before, cut, value.shape[0]), axis, -1)
    return value, after, low, high, before


def wide_shift(value, steps):
    count = lax.axis_size(("y", "x"))
    return lax.ppermute(
        value, ("y", "x"), [(i, i + steps) for i in range(max(0, -steps), min(count, count - steps))]
    )


def make_plan(tile_sector, term_charge, block_home, home, core, x, y):
    base = (y * 4 + x) * TILE_DEV
    paired = block_home.reshape(HOMES, TILE_DEV, 2)
    mine = jnp.where(core == 0, paired[:, :, 0], paired[:, :, 1])
    homes = home + jnp.arange(2, dtype=jnp.int32) * (1 - 2 * core)
    owner_ids = jnp.arange(HOMES, dtype=jnp.int32)[:, None, None]
    owner = jnp.sum(
        jnp.where(mine[:, :, None] == homes[None, None, :], owner_ids, 0), axis=0
    ).reshape(PAIRS)
    term = owner * 2 + core
    term_ids = jnp.arange(2 * HOMES, dtype=jnp.int32)
    charge = jnp.sum(jnp.where(term[:, None] == term_ids[None, :], term_charge[None, :], 0), axis=1)
    tiles = lax.dynamic_slice(tile_sector, (base,), (TILE_DEV,))
    source = jnp.broadcast_to(tiles[:, None], (TILE_DEV, 2)).reshape(PAIRS) + charge
    usable = (source >= 0) & (source <= tile_sector[-1])
    first = jnp.sum((tile_sector[None, :] < source[:, None]).astype(jnp.int32), axis=1)
    count = jnp.sum((tile_sector[None, :] == source[:, None]).astype(jnp.int32), axis=1)
    first = jnp.where(usable, first - (base - REACH * TILE_DEV), 0)
    count = jnp.where(usable, count, 0)
    slot = ((owner // 2 - home // 2) % (HOMES // 2)) * 2 + (owner + core) % 2
    return jnp.concatenate([first, count, slot, jnp.stack([core, x, y])]).astype(jnp.int32)


def on_device(wavefunction, env_blocks, right_env, tile_sector, term_charge, block_home):
    z, core = lax.axis_index("z"), lax.axis_index("core")
    y, x = lax.axis_index("y"), lax.axis_index("x")
    home = 2 * z + core
    swap = [(0, 1), (1, 0)]

    by_y = lax.dynamic_slice(right_env, (0, y * TILE + x * SUB, 0), (2, SUB, HALF))
    by_x = lax.dynamic_slice(right_env, (0, x * TILE + y * SUB, HALF), (2, SUB, HALF))
    strips = jnp.stack([by_y, by_x], axis=1)
    kept = lax.dynamic_index_in_dim(strips, core, axis=0, keepdims=False)
    given = lax.dynamic_index_in_dim(strips, 1 - core, axis=0, keepdims=False)
    strip = jnp.stack([kept, lax.ppermute(given, "core", swap)])
    column = {0: strip}
    for steps in (1, -1, 2, -2, 3, -3, 4):
        column[steps % 8] = ring(strip, "z", steps)

    strip = lax.dynamic_slice(wavefunction, (home * PART, 0), (PART, COLS))
    near = jnp.stack([wide_shift(strip, steps) for steps in (2, 1, -1, -2)])
    near = lax.all_gather(near, ("z", "core"))

    paired = env_blocks.reshape(TILE_DEV, 2, TILE, SRC)
    env_other = lax.ppermute(
        lax.dynamic_index_in_dim(paired, 1 - core, axis=1, keepdims=False), "core", swap
    )
    plan = make_plan(tile_sector, term_charge, block_home, home, core, x, y)

    env_other, column = lax.optimization_barrier((env_other, column))
    parts = []
    for at, (first, then) in enumerate((("x", "y"), ("y", "x"))):
        here, after, low, high, before = around(
            jnp.concatenate([column[steps][:, at] for steps in range(8)]), first, HOMES // 2
        )
        ahead = jnp.stack([here, after])
        behind = jnp.stack([jnp.concatenate([low, high], axis=0), before])
        ahead_after, behind_before = ring(ahead, then, 1), ring(behind, then, -1)
        across = ring(ahead_after, then, 1), ring(behind_before, then, -1)
        behind_late, ahead_after = lax.optimization_barrier((behind, ahead_after))
        ahead_late, behind_before = lax.optimization_barrier((ahead, behind_before))
        behind_after, ahead_before = ring(behind_late, then, 1), ring(ahead_late, then, -1)
        parts.append(
            ((ahead, behind), (ahead_after, behind_after), across, (ahead_before, behind_before))
        )

    left = left_products(plan, wavefunction, near, env_blocks, env_other)
    keep, send = right_products(plan, left, parts)
    total = keep + lax.ppermute(send, "core", swap)
    shares = lax.all_to_all(total, "z", split_axis=0, concat_axis=0, tiled=True)
    shares = shares.reshape(HOMES // 2, SUB, ROWS)
    return jnp.sum(shares, axis=0).T


def solution(mesh):
    fine = Mesh(mesh.devices.reshape(8, 2, 4, 4), ("z", "core", "y", "x"))
    bulk, wide = ("z", "core"), ("y", "x")
    return jax.shard_map(
        on_device,
        mesh=fine,
        in_specs=(P(wide, None), P(bulk, wide, None), P(bulk, None, None), P(), P(), P()),
        out_specs=P(wide, bulk),
        check_vma=False,
    )
```

```python
import jax
import jax.numpy as jnp
from jax import lax
from jax.experimental import pallas as pl
from jax.experimental.pallas import tpu as pltpu
from jax.sharding import Mesh, PartitionSpec as P

TILE = 128
COLS = 512
HALF = COLS // 2
TILE_DEV = 8
SRC = 1024
PAIRS = 16
HOMES = 16
REACH = 2
SLABS = 2 * REACH + 1
ROWS = TILE_DEV * TILE
PART = ROWS // HOMES
SUB = 32
DIRECT = 128
PACE = (COLS - DIRECT) // 4
STRIP = PACE // 4
VMEM = 56 * 1024 * 1024

START, COUNT, TERM, SLOT, CORE, PX, PY = 0, 16, 32, 48, 64, 65, 66


def split(value):
    high = value.astype(jnp.bfloat16)
    low = (value - high.astype(jnp.float32)).astype(jnp.bfloat16)
    return high, low


def product(left, high, low):
    left_high, left_low = split(left)
    rows = left.shape[0]
    both = jnp.dot(
        jnp.concatenate([left_high, left_low], axis=0), high, preferred_element_type=jnp.float32
    )
    rest = jnp.dot(left_high, low, preferred_element_type=jnp.float32)
    return both[:rows] + both[rows:] + rest


def left_kernel(plan, own, near, env_own, env_other, out, high, low):
    pair = pl.program_id(0)

    @pl.when(pair == 0)
    def _():
        def put(row, value):
            spot = pl.ds(pl.multiple_of(row, PART), PART)
            high[spot, :], low[spot, :] = split(value)

        @pl.loop(0, HOMES)
        def _(home):
            for at, slab in enumerate(s for s in range(SLABS) if s != REACH):
                put(slab * ROWS + home * PART, near[home, at])
            put(REACH * ROWS + home * PART, own[pl.ds(pl.multiple_of(home * PART, PART), PART), :])

        tail = jnp.zeros((2 * TILE, COLS), jnp.bfloat16)
        high[SLABS * ROWS :, :] = tail
        low[SLABS * ROWS :, :] = tail

    def contract(env):
        first, count = plan[START + pair], plan[COUNT + pair]
        out[0] = jnp.zeros((TILE, COLS), jnp.float32)

        def chunk(step, carry):
            block = env[0, :, pl.ds(pl.multiple_of(step * 2 * TILE, 2 * TILE), 2 * TILE)]
            column = step * 2 * TILE + lax.broadcasted_iota(jnp.int32, block.shape, 1)
            block = jnp.where(column < count * TILE, block, 0.0)
            spot = pl.ds(pl.multiple_of((first + 2 * step) * TILE, TILE), 2 * TILE)
            out[0] += product(block, high[spot, :], low[spot, :])
            return carry

        lax.fori_loop(0, (count + 1) // 2, chunk, 0)

    @pl.when(pair % 2 == 0)
    def _():
        contract(env_own)

    @pl.when(pair % 2 == 1)
    def _():
        contract(env_other)


def left_products(plan, own, near, env, env_other):
    grid = pltpu.PrefetchScalarGridSpec(
        num_scalar_prefetch=1,
        grid=(PAIRS,),
        in_specs=[
            pl.BlockSpec((ROWS, COLS), lambda p, plan: (0, 0), pipeline_mode=pl.Buffered(1)),
            pl.BlockSpec(near.shape, lambda p, plan: (0, 0, 0, 0), pipeline_mode=pl.Buffered(1)),
            pl.BlockSpec((1, TILE, SRC), lambda p, plan: ((p // 2) * 2 + plan[CORE], 0, 0)),
            pl.BlockSpec((1, TILE, SRC), lambda p, plan: (p // 2, 0, 0)),
        ],
        out_specs=pl.BlockSpec((1, TILE, COLS), lambda p, plan: (p, 0, 0)),
        scratch_shapes=[pltpu.VMEM((SLABS * ROWS + 2 * TILE, COLS), jnp.bfloat16)] * 2,
    )
    return pl.pallas_call(
        left_kernel,
        grid_spec=grid,
        out_shape=jax.ShapeDtypeStruct((PAIRS, TILE, COLS), jnp.float32),
        compiler_params=pltpu.CompilerParams(vmem_limit_bytes=VMEM),
        cost_estimate=pl.CostEstimate(
            flops=6 * PAIRS * TILE * SRC * COLS, bytes_accessed=24 << 20, transcendentals=0
        ),
        name="left_products",
    )(plan, own, near, env, env_other)


def right_kernel(plan, left, direct, *refs):
    parts, (keep, send, total, whole) = refs[:10], refs[10:]
    pair = pl.program_id(0)
    core, x, y = plan[CORE], plan[PX], plan[PY]
    for half, (major, minor) in enumerate(((y, x), (x, y))):
        here, after, across_low, across_high, before = parts[5 * half : 5 * half + 5]
        pieces = [
            [here.at[i] for i in range(4)],
            [after.at[i] for i in range(4)],
            [across_low.at[0], across_low.at[1], across_high.at[0], across_high.at[1]],
            [before.at[i] for i in range(4)],
        ]
        for r in range(4):
            for i in range(4):
                row = ((major + r) % 4) * PACE + ((minor + i) % 4) * STRIP
                spot = pl.ds(pl.multiple_of(row, 8), STRIP)
                whole[spot, half * HALF : (half + 1) * HALF] = pieces[r][i][0]
    whole[COLS - DIRECT :, :] = direct[0]
    high, low = split(whole[...])
    value = product(left[0], high, low)

    @pl.when(pair % 2 == 0)
    def _():
        total[...] = value

    @pl.when(pair % 2 == 1)
    def _():
        turned = (total[...] + value).T.reshape(HOMES // 2, 2, SUB, TILE)
        keep[...] = jnp.where(core == 0, turned[:, 0], turned[:, 1])
        send[...] = jnp.where(core == 0, turned[:, 1], turned[:, 0])


def right_products(plan, left, direct, parts):
    def part_spec(part):
        return pl.BlockSpec((part.shape[0], 1, STRIP, HALF), lambda p, plan: (0, plan[TERM + p], 0, 0))

    out = jax.ShapeDtypeStruct((HOMES // 2, SUB, ROWS), jnp.float32)
    out_spec = pl.BlockSpec((HOMES // 2, SUB, TILE), lambda p, plan: (0, 0, p // 2))
    grid = pltpu.PrefetchScalarGridSpec(
        num_scalar_prefetch=1,
        grid=(PAIRS,),
        in_specs=[
            pl.BlockSpec((1, TILE, COLS), lambda p, plan: (p, 0, 0)),
            pl.BlockSpec((1, DIRECT, COLS), lambda p, plan: (plan[SLOT + p], 0, 0)),
        ]
        + [part_spec(part) for part in parts],
        out_specs=[out_spec, out_spec],
        scratch_shapes=[
            pltpu.VMEM((TILE, COLS), jnp.float32),
            pltpu.VMEM((COLS, COLS), jnp.float32),
        ],
    )
    return pl.pallas_call(
        right_kernel,
        grid_spec=grid,
        out_shape=[out, out],
        compiler_params=pltpu.CompilerParams(vmem_limit_bytes=VMEM),
        cost_estimate=pl.CostEstimate(
            flops=6 * PAIRS * TILE * COLS * COLS, bytes_accessed=22 << 20, transcendentals=0
        ),
        name="right_products",
    )(plan, left, direct, *parts)


def ring(value, axis, steps):
    count = lax.axis_size(axis)
    return lax.ppermute(value, axis, [(i, (i - steps) % count) for i in range(count)])


def around(value, axis, cut):
    after, before = ring(value, axis, 1), ring(value, axis, -1)
    low = ring(lax.slice_in_dim(after, 0, cut), axis, 1)
    high = ring(lax.slice_in_dim(before, cut, value.shape[0]), axis, -1)
    return value, after, low, high, before


def wide_shift(value, steps):
    count = lax.axis_size(("y", "x"))
    return lax.ppermute(
        value, ("y", "x"), [(i, i + steps) for i in range(max(0, -steps), min(count, count - steps))]
    )


def make_plan(tile_sector, term_charge, block_home, home, core, x, y):
    base = (y * 4 + x) * TILE_DEV
    paired = block_home.reshape(HOMES, TILE_DEV, 2)
    mine = jnp.where(core == 0, paired[:, :, 0], paired[:, :, 1])
    homes = home + jnp.arange(2, dtype=jnp.int32) * (1 - 2 * core)
    owner_ids = jnp.arange(HOMES, dtype=jnp.int32)[:, None, None]
    owner = jnp.sum(
        jnp.where(mine[:, :, None] == homes[None, None, :], owner_ids, 0), axis=0
    ).reshape(PAIRS)
    term = owner * 2 + core
    term_ids = jnp.arange(2 * HOMES, dtype=jnp.int32)
    charge = jnp.sum(jnp.where(term[:, None] == term_ids[None, :], term_charge[None, :], 0), axis=1)
    tiles = lax.dynamic_slice(tile_sector, (base,), (TILE_DEV,))
    source = jnp.broadcast_to(tiles[:, None], (TILE_DEV, 2)).reshape(PAIRS) + charge
    usable = (source >= 0) & (source <= tile_sector[-1])
    first = jnp.sum((tile_sector[None, :] < source[:, None]).astype(jnp.int32), axis=1)
    count = jnp.sum((tile_sector[None, :] == source[:, None]).astype(jnp.int32), axis=1)
    first = jnp.where(usable, first - (base - REACH * TILE_DEV), 0)
    count = jnp.where(usable, count, 0)
    slot = (owner // 2) * 2 + (owner + core) % 2
    return jnp.concatenate([first, count, owner, slot, jnp.stack([core, x, y])]).astype(jnp.int32)


def on_device(wavefunction, env_blocks, right_env, tile_sector, term_charge, block_home):
    z, core = lax.axis_index("z"), lax.axis_index("core")
    y, x = lax.axis_index("y"), lax.axis_index("x")
    home = 2 * z + core
    swap = [(0, 1), (1, 0)]

    by_y = lax.dynamic_slice(right_env, (0, y * PACE + x * STRIP, 0), (2, STRIP, HALF))
    by_x = lax.dynamic_slice(right_env, (0, x * PACE + y * STRIP, HALF), (2, STRIP, HALF))
    column = lax.all_gather(jnp.stack([by_y, by_x], axis=1), ("z", "core"))

    strip = lax.dynamic_slice(wavefunction, (home * PART, 0), (PART, COLS))
    near = jnp.stack([wide_shift(strip, steps) for steps in (2, 1, -1, -2)])
    near, column = lax.optimization_barrier((near, column))
    near = lax.all_gather(near, ("z", "core"))

    rest = right_env[:, COLS - DIRECT :, :]
    kept = lax.dynamic_index_in_dim(rest, core, axis=0, keepdims=False)
    given = lax.dynamic_index_in_dim(rest, 1 - core, axis=0, keepdims=False)
    direct = jnp.stack([kept, lax.ppermute(given, "core", swap)])

    paired = env_blocks.reshape(TILE_DEV, 2, TILE, SRC)
    env_other = lax.ppermute(
        lax.dynamic_index_in_dim(paired, 1 - core, axis=1, keepdims=False), "core", swap
    )
    plan = make_plan(tile_sector, term_charge, block_home, home, core, x, y)

    mine = lax.dynamic_index_in_dim(column, core, axis=1, keepdims=False)
    parts = []
    for at, (first, then) in enumerate((("x", "y"), ("y", "x"))):
        here, after, low, high, before = around(mine[:, at], first, HOMES // 2)
        if at == 0:
            direct, after = lax.optimization_barrier((direct, after))
            direct = lax.all_gather(direct, "z").reshape(HOMES, DIRECT, COLS)
        gathered = jnp.stack([here, after, jnp.concatenate([low, high], axis=0), before])
        parts += around(gathered, then, 2)

    left = left_products(plan, wavefunction, near, env_blocks, env_other)
    keep, send = right_products(plan, left, direct, parts)
    total = keep + lax.ppermute(send, "core", swap)
    shares = lax.all_to_all(total, "z", split_axis=0, concat_axis=0, tiled=True)
    shares = shares.reshape(HOMES // 2, SUB, ROWS)
    return jnp.sum(shares, axis=0).T


def solution(mesh):
    fine = Mesh(mesh.devices.reshape(8, 2, 4, 4), ("z", "core", "y", "x"))
    bulk, wide = ("z", "core"), ("y", "x")
    return jax.shard_map(
        on_device,
        mesh=fine,
        in_specs=(P(wide, None), P(bulk, wide, None), P(bulk, None, None), P(), P(), P()),
        out_specs=P(wide, bulk),
        check_vma=False,
    )
```

```python
import jax
import jax.numpy as jnp
from jax import lax
from jax.experimental import pallas as pl
from jax.experimental.pallas import tpu as pltpu
from jax.sharding import Mesh, PartitionSpec as P

TILE = 128
COLS = 512
HALF = COLS // 2
TILE_DEV = 8
SRC = 1024
PAIRS = 16
HOMES = 16
REACH = 2
SLABS = 2 * REACH + 1
ROWS = TILE_DEV * TILE
PART = ROWS // HOMES
SUB = 32
VMEM = 56 * 1024 * 1024

START, COUNT, TERM, CORE, PX, PY = 0, 16, 32, 48, 49, 50


def split(value):
    high = value.astype(jnp.bfloat16)
    low = (value - high.astype(jnp.float32)).astype(jnp.bfloat16)
    return high, low


def product(left, high, low):
    left_high, left_low = split(left)
    rows = left.shape[0]
    both = jnp.dot(
        jnp.concatenate([left_high, left_low], axis=0), high, preferred_element_type=jnp.float32
    )
    rest = jnp.dot(left_high, low, preferred_element_type=jnp.float32)
    return both[:rows] + both[rows:] + rest


def left_kernel(plan, own, near, env_own, env_other, out, high, low):
    pair = pl.program_id(0)

    @pl.when(pair == 0)
    def _():
        def put(row, value):
            spot = pl.ds(pl.multiple_of(row, PART), PART)
            high[spot, :], low[spot, :] = split(value)

        @pl.loop(0, HOMES)
        def _(home):
            for at, slab in enumerate(s for s in range(SLABS) if s != REACH):
                put(slab * ROWS + home * PART, near[home, at])
            put(REACH * ROWS + home * PART, own[pl.ds(pl.multiple_of(home * PART, PART), PART), :])

        tail = jnp.zeros((2 * TILE, COLS), jnp.bfloat16)
        high[SLABS * ROWS :, :] = tail
        low[SLABS * ROWS :, :] = tail

    def contract(env):
        first, count = plan[START + pair], plan[COUNT + pair]
        out[0] = jnp.zeros((TILE, COLS), jnp.float32)

        def chunk(step, carry):
            block = env[0, :, pl.ds(pl.multiple_of(step * 2 * TILE, 2 * TILE), 2 * TILE)]
            column = step * 2 * TILE + lax.broadcasted_iota(jnp.int32, block.shape, 1)
            block = jnp.where(column < count * TILE, block, 0.0)
            spot = pl.ds(pl.multiple_of((first + 2 * step) * TILE, TILE), 2 * TILE)
            out[0] += product(block, high[spot, :], low[spot, :])
            return carry

        lax.fori_loop(0, (count + 1) // 2, chunk, 0)

    @pl.when(pair % 2 == 0)
    def _():
        contract(env_own)

    @pl.when(pair % 2 == 1)
    def _():
        contract(env_other)


def left_products(plan, own, near, env, env_other):
    grid = pltpu.PrefetchScalarGridSpec(
        num_scalar_prefetch=1,
        grid=(PAIRS,),
        in_specs=[
            pl.BlockSpec((ROWS, COLS), lambda p, plan: (0, 0), pipeline_mode=pl.Buffered(1)),
            pl.BlockSpec(near.shape, lambda p, plan: (0, 0, 0, 0), pipeline_mode=pl.Buffered(1)),
            pl.BlockSpec((1, TILE, SRC), lambda p, plan: ((p // 2) * 2 + plan[CORE], 0, 0)),
            pl.BlockSpec((1, TILE, SRC), lambda p, plan: (p // 2, 0, 0)),
        ],
        out_specs=pl.BlockSpec((1, TILE, COLS), lambda p, plan: (p, 0, 0)),
        scratch_shapes=[pltpu.VMEM((SLABS * ROWS + 2 * TILE, COLS), jnp.bfloat16)] * 2,
    )
    return pl.pallas_call(
        left_kernel,
        grid_spec=grid,
        out_shape=jax.ShapeDtypeStruct((PAIRS, TILE, COLS), jnp.float32),
        compiler_params=pltpu.CompilerParams(vmem_limit_bytes=VMEM),
        cost_estimate=pl.CostEstimate(
            flops=6 * PAIRS * TILE * SRC * COLS, bytes_accessed=24 << 20, transcendentals=0
        ),
        name="left_products",
    )(plan, own, near, env, env_other)


def right_kernel(plan, left, *refs):
    parts, (keep, send, total, *halves) = refs[:10], refs[10:]
    pair = pl.program_id(0)
    core, x, y = plan[CORE], plan[PX], plan[PY]
    value = []
    for half, (major, minor) in enumerate(((y, x), (x, y))):
        here, after, across_low, across_high, before = parts[5 * half : 5 * half + 5]
        high, low = halves[2 * half : 2 * half + 2]
        pieces = [
            [here.at[i] for i in range(4)],
            [after.at[i] for i in range(4)],
            [across_low.at[0], across_low.at[1], across_high.at[0], across_high.at[1]],
            [before.at[i] for i in range(4)],
        ]
        lefts = []
        for r in range(4):
            for i in range(4):
                spot = pl.ds(pl.multiple_of(r * TILE + ((minor + i) % 4) * SUB, SUB), SUB)
                high[spot, :], low[spot, :] = split(pieces[r][i][0])
            lefts.append(left[0, :, pl.ds(pl.multiple_of(((major + r) % 4) * TILE, TILE), TILE)])
        value.append(product(jnp.concatenate(lefts, axis=1), high[...], low[...]))
    value = jnp.concatenate(value, axis=1)

    @pl.when(pair % 2 == 0)
    def _():
        total[...] = value

    @pl.when(pair % 2 == 1)
    def _():
        turned = (total[...] + value).T.reshape(HOMES // 2, 2, SUB, TILE)
        keep[...] = jnp.where(core == 0, turned[:, 0], turned[:, 1])
        send[...] = jnp.where(core == 0, turned[:, 1], turned[:, 0])


def right_products(plan, left, parts):
    def part_spec(part):
        return pl.BlockSpec((part.shape[0], 1, SUB, HALF), lambda p, plan: (0, plan[TERM + p], 0, 0))

    out = jax.ShapeDtypeStruct((HOMES // 2, SUB, ROWS), jnp.float32)
    out_spec = pl.BlockSpec((HOMES // 2, SUB, TILE), lambda p, plan: (0, 0, p // 2))
    grid = pltpu.PrefetchScalarGridSpec(
        num_scalar_prefetch=1,
        grid=(PAIRS,),
        in_specs=[pl.BlockSpec((1, TILE, COLS), lambda p, plan: (p, 0, 0))]
        + [part_spec(part) for part in parts],
        out_specs=[out_spec, out_spec],
        scratch_shapes=[pltpu.VMEM((TILE, COLS), jnp.float32)]
        + [pltpu.VMEM((COLS, HALF), jnp.bfloat16)] * 4,
    )
    return pl.pallas_call(
        right_kernel,
        grid_spec=grid,
        out_shape=[out, out],
        compiler_params=pltpu.CompilerParams(vmem_limit_bytes=VMEM),
        cost_estimate=pl.CostEstimate(
            flops=6 * PAIRS * TILE * COLS * COLS, bytes_accessed=22 << 20, transcendentals=0
        ),
        name="right_products",
    )(plan, left, *parts)


def ring(value, axis, steps):
    count = lax.axis_size(axis)
    return lax.ppermute(value, axis, [(i, (i - steps) % count) for i in range(count)])


def around(value, axis, cut):
    after, before = ring(value, axis, 1), ring(value, axis, -1)
    low = ring(lax.slice_in_dim(after, 0, cut), axis, 1)
    high = ring(lax.slice_in_dim(before, cut, value.shape[0]), axis, -1)
    return value, after, low, high, before


def wide_shift(value, steps):
    count = lax.axis_size(("y", "x"))
    return lax.ppermute(
        value, ("y", "x"), [(i, i + steps) for i in range(max(0, -steps), min(count, count - steps))]
    )


def make_plan(tile_sector, term_charge, block_home, home, core, x, y):
    base = (y * 4 + x) * TILE_DEV
    paired = block_home.reshape(HOMES, TILE_DEV, 2)
    mine = jnp.where(core == 0, paired[:, :, 0], paired[:, :, 1])
    homes = home + jnp.arange(2, dtype=jnp.int32) * (1 - 2 * core)
    owner_ids = jnp.arange(HOMES, dtype=jnp.int32)[:, None, None]
    owner = jnp.sum(
        jnp.where(mine[:, :, None] == homes[None, None, :], owner_ids, 0), axis=0
    ).reshape(PAIRS)
    term = owner * 2 + core
    term_ids = jnp.arange(2 * HOMES, dtype=jnp.int32)
    charge = jnp.sum(jnp.where(term[:, None] == term_ids[None, :], term_charge[None, :], 0), axis=1)
    tiles = lax.dynamic_slice(tile_sector, (base,), (TILE_DEV,))
    source = jnp.broadcast_to(tiles[:, None], (TILE_DEV, 2)).reshape(PAIRS) + charge
    usable = (source >= 0) & (source <= tile_sector[-1])
    first = jnp.sum((tile_sector[None, :] < source[:, None]).astype(jnp.int32), axis=1)
    count = jnp.sum((tile_sector[None, :] == source[:, None]).astype(jnp.int32), axis=1)
    first = jnp.where(usable, first - (base - REACH * TILE_DEV), 0)
    count = jnp.where(usable, count, 0)
    return jnp.concatenate([first, count, owner, jnp.stack([core, x, y])]).astype(jnp.int32)


def on_device(wavefunction, env_blocks, right_env, tile_sector, term_charge, block_home):
    z, core = lax.axis_index("z"), lax.axis_index("core")
    y, x = lax.axis_index("y"), lax.axis_index("x")
    home = 2 * z + core
    swap = [(0, 1), (1, 0)]

    by_y = lax.dynamic_slice(right_env, (0, y * TILE + x * SUB, 0), (2, SUB, HALF))
    by_x = lax.dynamic_slice(right_env, (0, x * TILE + y * SUB, HALF), (2, SUB, HALF))
    column = lax.all_gather(jnp.stack([by_y, by_x], axis=1), ("z", "core"))

    strip = lax.dynamic_slice(wavefunction, (home * PART, 0), (PART, COLS))
    near = jnp.stack([wide_shift(strip, steps) for steps in (2, 1, -1, -2)])
    near = lax.all_gather(near, ("z", "core"))

    paired = env_blocks.reshape(TILE_DEV, 2, TILE, SRC)
    env_other = lax.ppermute(
        lax.dynamic_index_in_dim(paired, 1 - core, axis=1, keepdims=False), "core", swap
    )
    plan = make_plan(tile_sector, term_charge, block_home, home, core, x, y)

    env_other, column = lax.optimization_barrier((env_other, column))
    mine = lax.dynamic_index_in_dim(column, core, axis=1, keepdims=False)
    parts = []
    for at, (first, then) in enumerate((("x", "y"), ("y", "x"))):
        here, after, low, high, before = around(mine[:, at], first, HOMES // 2)
        gathered = jnp.stack([here, after, jnp.concatenate([low, high], axis=0), before])
        parts += around(gathered, then, 2)

    left = left_products(plan, wavefunction, near, env_blocks, env_other)
    keep, send = right_products(plan, left, parts)
    total = keep + lax.ppermute(send, "core", swap)
    shares = lax.all_to_all(total, "z", split_axis=0, concat_axis=0, tiled=True)
    shares = shares.reshape(HOMES // 2, SUB, ROWS)
    return jnp.sum(shares, axis=0).T


def solution(mesh):
    fine = Mesh(mesh.devices.reshape(8, 2, 4, 4), ("z", "core", "y", "x"))
    bulk, wide = ("z", "core"), ("y", "x")
    return jax.shard_map(
        on_device,
        mesh=fine,
        in_specs=(P(wide, None), P(bulk, wide, None), P(bulk, None, None), P(), P(), P()),
        out_specs=P(wide, bulk),
        check_vma=False,
    )
```
